128 devices in a mesh: energy: 8 (over z, core), cuts: 16 (over y, x).
Axes of the slice: x: 4, y: 4, z: 4, core: 2. Of those that a mesh axis runs over, the one named last changes fastest.
Arguments:
- coupling: bfloat16 [16, 720, 720], P('cuts'), may hold values from -0.3125 to 0.3125
- block_mask: int32 [16, 6, 6], P('cuts'), may hold values from 0 to 1, as said below
- levels: float32 [16, 720], P('cuts'), may hold values from -4 to 4
- dwell: float32 [16, 720], P('cuts'), may hold values from 0.5 to 3
- polarization: bfloat16 [2, 16, 16, 720, 720], P(None, 'energy', 'cuts'), may hold values from -6 to 6
Outputs:
- sigma: bfloat16 [2, 16, 16, 720, 720], P(None, 'energy', 'cuts')
The draws below stay inside these ranges and needn't reach their ends.
Inputs may be any that keep to these rules, and one draw needn't show every extreme that they name: `block_mask`: 1 where a coupling block of a slice is present, else 0; the diagonal blocks are always present.
All inputs are finite; a program needn't handle non-finite values.
Results may differ from the reference program's by a relative error of at most 0.023.
Values may be sent and summed in bfloat16 or wider, within the bound.
A program may use at most 192 MiB of HBM per device.

```python
import math
import jax
import jax.numpy as jnp
from jax import lax

NO = 720
BLOCKS = 6
NE = 16
SLICES = 16


def draw_block_mask(key, part):
    random_bits = jax.random.randint(key, (SLICES, BLOCKS, BLOCKS), 0, 2)
    diagonal = jnp.eye(BLOCKS, dtype=jnp.int32)
    return jnp.maximum(random_bits, diagonal[None]).astype(jnp.int32)


def block_levels(key, extent, pieces, smallest, top_value):
    def one(position, shards_of):
        draws = jax.random.uniform(jax.random.fold_in(jax.random.fold_in(key, 6), position), (shards_of,), jnp.float32, smallest / len(pieces), top_value / len(pieces))
        return jnp.repeat(jnp.exp(draws), extent[position] // shards_of).reshape((-1,) + (1,) * (len(extent) - position - 1))

    level = one(*pieces[0])
    for cut in pieces[1:]:
        level = level * one(*cut)
    return level


def centred(own_key, extent, width, bound, pieces=(), kind=jnp.bfloat16):
    array = width * jax.random.normal(own_key, extent, jnp.float32)
    if pieces:
        array = array * block_levels(own_key, extent, pieces, -0.22, 0.18)
    return jnp.clip(array, -bound, bound).astype(kind)


def setup_inputs(seed: int = 0) -> dict:
    splits = jax.random.split(jax.random.key(seed), 6)
    coupling = centred(splits[0], (SLICES, NO, NO), (NO * 7 // 12) ** -0.5, 0.3125, ((0, 16),))
    block_mask = draw_block_mask(jax.random.fold_in(splits[5], 71), 0)
    levels = jnp.clip(jax.random.uniform(splits[2], (SLICES, NO), jnp.float32, -4.0, 4.0) * block_levels(splits[2], (SLICES, NO), ((0, 16),), -0.4, 0.0), -4.0, 4.0)
    dwell = jnp.clip(jnp.exp(math.log(3.0) - 1.7917595 * jax.random.uniform(splits[3], (SLICES, NO), jnp.float32) ** block_levels(splits[3], (SLICES, NO), ((0, 16),), -0.2, 0.2)), 0.5, 3.0)
    polarization = centred(splits[4], (2, NE, SLICES, NO, NO), 1.0, 6.0, ((1, 8), (2, 16)))
    return {"coupling": coupling, "block_mask": block_mask, "levels": levels, "dwell": dwell, "polarization": polarization}


def complex_step(left_real, left_imag, right_real, right_imag):
    left_real = left_real.astype(jnp.float32)
    left_imag = left_imag.astype(jnp.float32)
    right_real = right_real.astype(jnp.float32)
    right_imag = right_imag.astype(jnp.float32)
    real_part = jnp.einsum('eab,ebc->eac', left_real, right_real) - jnp.einsum('eab,ebc->eac', left_imag, right_imag)
    imag_part = jnp.einsum('eab,ebc->eac', left_real, right_imag) + jnp.einsum('eab,ebc->eac', left_imag, right_real)
    return (real_part.astype(jnp.bfloat16), imag_part.astype(jnp.bfloat16))

def convolve_direct(green_real, green_imag, polar_block):
    energy_count = green_real.shape[0]
    green_real = green_real.astype(jnp.float32)
    green_imag = green_imag.astype(jnp.float32)
    polar_real = polar_block[0].astype(jnp.float32)
    polar_imag = polar_block[1].astype(jnp.float32)
    total_real = jnp.zeros(green_real.shape, jnp.float32)
    total_imag = jnp.zeros(green_real.shape, jnp.float32)
    for offset in range(energy_count):
        shift_real = jnp.pad(green_real[:energy_count - offset], ((offset, 0), (0, 0), (0, 0)))
        shift_imag = jnp.pad(green_imag[:energy_count - offset], ((offset, 0), (0, 0), (0, 0)))
        total_real = total_real + shift_real * polar_real[offset] - shift_imag * polar_imag[offset]
        total_imag = total_imag + shift_real * polar_imag[offset] + shift_imag * polar_real[offset]
    factor = math.sqrt(NO / NE)
    return (jnp.stack([total_real, total_imag]) * factor).astype(jnp.bfloat16)

def reference(coupling, block_mask, levels, dwell, polarization):
    block_width = NO // block_mask.shape[1]
    energy = jnp.arange(NE).astype(jnp.float32)

    def slice_step(propagator, inputs):
        couple, mask_small, level_row, dwell_row, polar_block = inputs
        spread_mask = jnp.repeat(jnp.repeat(mask_small, block_width, axis=0), block_width, axis=1)
        masked = couple.astype(jnp.float32) * spread_mask.astype(jnp.float32)
        phases = (energy[:, None] - level_row[None, :]) * dwell_row[None, :]
        step_re = (jnp.cos(phases)[:, :, None] * masked[None]).astype(jnp.bfloat16)
        step_im = (-jnp.sin(phases)[:, :, None] * masked[None]).astype(jnp.bfloat16)
        green_real, green_imag = complex_step(step_re, step_im, propagator[0], propagator[1])
        sigma_block = convolve_direct(green_real, green_imag, polar_block)
        return ((green_real, green_imag), sigma_block)
    identity_tile = jnp.broadcast_to(jnp.eye(NO, dtype=jnp.bfloat16), (NE, NO, NO))
    start = (identity_tile, jnp.zeros((NE, NO, NO), jnp.bfloat16))
    polar_slices = jnp.moveaxis(polarization, 2, 0)
    final, sigma_slices = lax.scan(slice_step, start, (coupling, block_mask, levels, dwell, polar_slices))
    return jnp.moveaxis(sigma_slices, 0, 2)
```

```python
import functools
import math

import jax
import jax.numpy as jnp
from jax import lax
from jax.experimental import pallas as pl
from jax.experimental.pallas import tpu as pltpu
from jax.sharding import PartitionSpec as P

MESH = pl.DeviceIdType.MESH
F32 = jnp.float32
BF16 = jnp.bfloat16

NX = 4
NY = 4
NG = 8
NI = NX * NY
ROWS = 96
CH = 16
H0 = 320
SPREAD = (0, 2)
GA = 64
EB = 8
EC = 16


def row_start(g, n):
    return jnp.minimum(g * ROWS, n - ROWS)


def pairwise(parts, value):
    rank = 0
    while parts and parts[-1][0] == rank:
        value = parts.pop()[1] + value
        rank += 1
    parts.append((rank, value))


def collect(parts):
    total = parts.pop()[1]
    while parts:
        total = parts.pop()[1] + total
    return total


def kernel(
    coup, mask, lev, dwl, pol, out,
    call, lall, dall, tab, rph, x, p, sig,
    a_send, a_recv, b_send, b_recv, f_send, c_send, c_recv, l_send, l_recv,
    p_send, p_recv, o_send, o_recv, loc,
):
    n = coup.shape[1]
    ne = x.shape[0]
    nch = ROWS // CH
    g = lax.axis_index("energy")
    i = lax.axis_index("cuts")
    core = g % 2
    yy = i // NX
    xx = i % NX
    r0 = pl.multiple_of(row_start(g, n), 16)

    barrier = pltpu.get_barrier_semaphore()
    for d in range(1, NG):
        pl.semaphore_signal(barrier, 1, device_id=((g + d) % NG, i), device_id_type=MESH)
    for d in range(1, NI):
        pl.semaphore_signal(barrier, 1, device_id=(g, (i + d) % NI), device_id_type=MESH)

    nb = mask.shape[0]
    bw = n // nb
    left = (
        lax.broadcasted_iota(jnp.int32, (n, nb), 0) // bw
        == lax.broadcasted_iota(jnp.int32, (n, nb), 1)
    ).astype(F32).astype(BF16)
    right = (
        lax.broadcasted_iota(jnp.int32, (nb, n), 1) // bw
        == lax.broadcasted_iota(jnp.int32, (nb, n), 0)
    ).astype(F32).astype(BF16)
    small = mask[:, 0, :].astype(F32).astype(BF16)
    wide = jnp.dot(small, right, preferred_element_type=F32).astype(BF16)
    spread = jnp.dot(left, wide, preferred_element_type=F32)
    call[i] = (coup[0].astype(F32) * spread).astype(BF16)

    pl.semaphore_wait(barrier, NG - 1 + NI - 1)

    def share_rows(k):
        return pl.ds(0, H0) if k == 0 else pl.ds(H0, n - H0)

    class Share:
        def __init__(self, make, other=False):
            self.make = make
            self.other = other

        def each(self, act):
            for k in range(2):
                rows = share_rows(1 - k if self.other else k)
                pl.when(core == k)(functools.partial(act, rows))

        def start(self):
            self.each(lambda rows: self.make(rows).start())

        def wait(self):
            self.each(lambda rows: self.make(rows).wait())

        def wait_send(self):
            self.each(lambda rows: self.make(rows).wait_send())

    def send_half(j, dest, ssem, rsem):
        return Share(
            lambda rows: pltpu.make_async_remote_copy(
                call.at[j, rows, :], call.at[j, rows, :], ssem, rsem,
                device_id=(g, dest), device_id_type=MESH,
            )
        )

    def arrived(j, sem, other=False):
        Share(
            lambda rows: pltpu.make_async_copy(
                call.at[j, rows, :], call.at[j, rows, :], sem
            ),
            other,
        ).wait()

    def l_copy(src, dst, k, dest):
        return pltpu.make_async_remote_copy(
            src, dst.at[i], l_send.at[k, dest], l_recv.at[k, i],
            device_id=(g, dest), device_id_type=MESH,
        )

    def l_start(d, _):
        dest = (i + d) % NI
        l_copy(lev, lall, 0, dest).start()
        l_copy(dwl, dall, 1, dest).start()
        return 0

    lax.fori_loop(1, NI, l_start, 0)

    relays = jnp.logical_and(core == 0, yy < NY - 1)

    def row_mate(d):
        return yy * NX + (xx + d) % NX

    for d in (1, 3, 2):
        ok = jnp.logical_or(relays, xx + d < NX)

        @pl.when(ok)
        def _():
            send_half(i, row_mate(d), a_send.at[0, d], a_recv.at[i]).start()

    def column_send(d):
        send_half(i, i + d * NX, a_send.at[1, d], a_recv.at[i]).start()

    for d in (1, 3):
        pl.when(yy + d < NY)(functools.partial(column_send, d))
    pl.when(jnp.logical_and(core == 1, yy + 2 < NY))(functools.partial(column_send, 2))

    def p_copy(d):
        dest = (g + d) % NG
        rd = pl.multiple_of(row_start(dest, n), 16)
        return pltpu.make_async_remote_copy(
            pol.at[:, :, 0, pl.ds(rd, ROWS), :], p.at[:, pl.ds(2 * g, 2)],
            p_send.at[d], p_recv.at[g], device_id=(dest, i), device_id_type=MESH,
        )

    for d in range(1, NG):
        p_copy(d).start()
    p_own = pltpu.make_async_copy(
        pol.at[:, :, 0, pl.ds(r0, ROWS), :], p.at[:, pl.ds(2 * g, 2)], p_recv.at[g]
    )
    p_own.start()

    lall[i] = lev[...]
    dall[i] = dwl[...]

    def l_wait(d, _):
        src = (i + d) % NI
        pltpu.make_async_copy(lall.at[src], lall.at[src], l_recv.at[0, src]).wait()
        pltpu.make_async_copy(dall.at[src], dall.at[src], l_recv.at[1, src]).wait()
        return 0

    lax.fori_loop(1, NI, l_wait, 0)

    tab[0, 0] = jnp.ones((ne, n), F32)
    tab[0, 1] = jnp.zeros((ne, n), F32)
    energy = lax.broadcasted_iota(jnp.int32, (ne, n), 0).astype(F32)

    def tables(j, _):
        phase = (energy - lall[j]) * dall[j]
        tab[j + 1, 0] = jnp.cos(phase)
        tab[j + 1, 1] = jnp.sin(phase)
        return 0

    lax.fori_loop(0, i, tables, 0)

    def share(j):
        return Share(
            lambda rows: pltpu.make_async_remote_copy(
                call.at[j, rows, :], call.at[j, rows, :], c_send.at[j], c_recv.at[j],
                device_id=(g + 1 - 2 * core, i), device_id_type=MESH,
            )
        )

    def own_line(j):
        return jnp.where(core == 0, j // NX == yy, j % NX == xx)

    def relay(j, dest):
        return send_half(j, dest, f_send.at[j], b_recv.at[j])

    @pl.when(core == 0)
    def _():
        @pl.when(yy == 1)
        def _():
            send_half(i, i - NX, a_send.at[1, 2], b_recv.at[i]).start()

        for d in (1, 3):
            j = yy * NX + (xx + NX - d) % NX

            @pl.when(jnp.logical_or(relays, j < i))
            def _():
                arrived(j, a_recv.at[j])

            @pl.when(j < i)
            def _():
                share(j).start()

            for k in (1, 3):

                @pl.when(yy + k < NY)
                def _():
                    send_half(j, i + k * NX, b_send.at[d, k], b_recv.at[j]).start()

            if d == 1:

                @pl.when(yy == 1)
                def _():
                    send_half(j, i - NX, b_send.at[d, 2], b_recv.at[j]).start()

        @pl.when(yy == 0)
        def _():
            for d in (0, 1):
                j = NX + (xx + NX - d) % NX
                arrived(j, b_recv.at[j])
                relay(j, i + 3 * NX).start()

    def spread_row(d):
        @pl.when(jnp.logical_and(core == 1, yy >= d))
        def _():
            j = i - d * NX
            arrived(j, a_recv.at[j])
            share(j).start()
            for k in (1, 3, 2):
                send_half(j, row_mate(k), b_send.at[d, k], b_recv.at[j]).start()

    spread_row(1)

    pick = (
        lax.broadcasted_iota(jnp.int32, (ROWS, n), 1)
        == lax.broadcasted_iota(jnp.int32, (ROWS, n), 0) + r0
    )
    col_lev = jnp.sum(jnp.where(pick, lev[...], 0.0), axis=1, keepdims=True)
    col_dwl = jnp.sum(jnp.where(pick, dwl[...], 0.0), axis=1, keepdims=True)
    col_phase = (
        lax.broadcasted_iota(jnp.int32, (ROWS, ne), 1).astype(F32) - col_lev
    ) * col_dwl
    rph[0] = jnp.cos(col_phase)
    rph[1] = jnp.sin(col_phase)

    def init(e, _):
        lane = lax.broadcasted_iota(jnp.int32, (ROWS, ne), 1) == e
        rc = jnp.sum(jnp.where(lane, rph[0], 0.0), axis=1, keepdims=True)
        rs = jnp.sum(jnp.where(lane, rph[1], 0.0), axis=1, keepdims=True)
        c = tab[i, 0, pl.ds(e, 1), :]
        s = tab[i, 1, pl.ds(e, 1), :]
        base = call[i, pl.ds(r0, ROWS), :].astype(F32) * math.sqrt(n / ne)
        x[e, 0] = (base * (rc * c - rs * s)).astype(BF16)
        x[e, 1] = (-base * (rc * s + rs * c)).astype(BF16)
        return 0

    lax.fori_loop(0, ne, init, 0)

    def late():
        j = yy * NX + (xx + 2) % NX

        @pl.when(jnp.logical_or(relays, j < i))
        def _():
            arrived(j, a_recv.at[j])

        @pl.when(j < i)
        def _():
            share(j).start()

        for k in (1, 3):

            @pl.when(yy + k < NY)
            def _():
                send_half(j, i + k * NX, b_send.at[2, k], b_recv.at[j]).start()

    def passes(j):
        first = jnp.logical_and(yy == 1, j // NX == 0)
        second = jnp.logical_and(yy == 2, jnp.logical_and(j // NX == 1, (xx + NX - j % NX) % NX >= 2))
        return jnp.logical_and(core == 0, jnp.logical_or(first, second))

    def take(j):
        @pl.when(jnp.logical_not(own_line(j)))
        def _():
            direct = jnp.where(
                core == 0,
                jnp.logical_and(j % NX == xx, yy - j // NX != 2),
                j // NX == yy,
            )

            @pl.when(direct)
            def _():
                arrived(j, a_recv.at[j])

            @pl.when(jnp.logical_not(direct))
            def _():
                arrived(j, b_recv.at[j])

            @pl.when(passes(j))
            def _():
                relay(j, i + NX).start()

            share(j).start()

    @pl.when(jnp.logical_and(core == 0, i == 0))
    def _():
        late()

    @pl.when(i > 0)
    def _():
        take(i - 1)


    def block(j, b, rows, count):
        first, size = rows
        z = x[pl.ds(b * count, count), :, first : first + size, :]
        z = z.reshape(count * 2 * size, n)
        r = jnp.dot(z, call[j], preferred_element_type=F32)
        for k in range(count):
            e = b * count + k
            c = tab[j, 0, pl.ds(e, 1), :]
            s = tab[j, 1, pl.ds(e, 1), :]
            re = r[2 * k * size : (2 * k + 1) * size]
            im = r[(2 * k + 1) * size : (2 * k + 2) * size]
            x[e, 0, first : first + size, :] = (re * c + im * s).astype(BF16)
            x[e, 1, first : first + size, :] = (im * c - re * s).astype(BF16)

    def chain(q, _):
        j = i - 1 - q
        arrived(j, c_recv.at[j], other=True)

        def part(b, _):
            block(j, b, (0, GA), EB)

            @pl.when(b == 0)
            def _():
                @pl.when(jnp.logical_and(core == 0, q == 0))
                def _():
                    late()

                for d in range(2, NY):
                    pl.when(q == SPREAD[d - 2])(functools.partial(spread_row, d))

                @pl.when(j > 0)
                def _():
                    take(j - 1)

            return 0

        lax.fori_loop(0, ne // EB, part, 0)
        return 0

    lax.fori_loop(0, i, chain, 0)

    def chain_rest(q, _):
        j = i - 1 - q

        def part(b, _):
            block(j, b, (GA, ROWS - GA), EC)
            return 0

        lax.fori_loop(0, ne // EC, part, 0)
        return 0

    p_own.wait()
    for d in range(1, NG):
        src = (g + NG - d) % NG
        view = p.at[:, pl.ds(2 * src, 2)]
        pltpu.make_async_copy(view, view, p_recv.at[src]).wait()

    def o_copy(d, q):
        dest = (g + d) % NG
        rows = pl.ds(pl.multiple_of(r0 + q * CH, CH), CH)
        return pltpu.make_async_remote_copy(
            sig.at[:, pl.ds(2 * dest, 2), pl.ds(pl.multiple_of(q * CH, CH), CH), :],
            out.at[:, :, 0, rows, :],
            o_send.at[d, q], o_recv.at[g, q], device_id=(dest, i), device_id_type=MESH,
        )

    def o_own(q):
        rows = pl.ds(pl.multiple_of(r0 + q * CH, CH), CH)
        return pltpu.make_async_copy(
            sig.at[:, pl.ds(2 * g, 2), pl.ds(pl.multiple_of(q * CH, CH), CH), :],
            out.at[:, :, 0, rows, :], loc.at[q],
        )

    q_first = (g * ROWS - r0) // CH

    def chunk(q, _):
        rows = pl.ds(pl.multiple_of(q * CH, CH), CH)

        def tile(lane):
            ga = [x[e, 0, rows, lane] for e in range(ne)]
            gb = [x[e, 1, rows, lane] for e in range(ne)]
            for e in range(ne):
                res, ims = [], []
                for w in range(e + 1):
                    pr = p[0, w, rows, lane]
                    pi = p[1, w, rows, lane]
                    pairwise(res, pr * ga[e - w] - pi * gb[e - w])
                    pairwise(ims, pr * gb[e - w] + pi * ga[e - w])
                sig[0, e, rows, lane] = collect(res)
                sig[1, e, rows, lane] = collect(ims)

        def whole(t, _):
            tile(pl.ds(pl.multiple_of(t * 128, 128), 128))
            return 0

        lax.fori_loop(0, n // 128, whole, 0)
        if n % 128:
            tile(pl.ds(n - n % 128, n % 128))
        for d in range(1, NG):
            o_copy(d, q).start()
        o_own(q).start()
        return 0

    lax.fori_loop(q_first, GA // CH, chunk, 0)
    lax.fori_loop(0, i, chain_rest, 0)
    lax.fori_loop(GA // CH, nch, chunk, 0)

    for d in range(1, NX):
        ok = jnp.logical_or(relays, xx + d < NX)

        @pl.when(ok)
        def _():
            send_half(i, row_mate(d), a_send.at[0, d], a_recv.at[i]).wait_send()

    def sent(sem):
        send_half(i, i, sem, a_recv.at[i]).wait_send()

    for d in (1, 3):
        pl.when(yy + d < NY)(functools.partial(sent, a_send.at[1, d]))
    ok = jnp.where(core == 1, yy + 2 < NY, yy == 1)
    pl.when(ok)(functools.partial(sent, a_send.at[1, 2]))
    for d in range(1, NX):
        for k in (1, 3):
            ok = jnp.where(core == 0, yy + k < NY, yy >= d)
            pl.when(ok)(functools.partial(sent, b_send.at[d, k]))
        ok = jnp.where(core == 0, yy == 1 if d == 1 else False, yy >= d)
        pl.when(ok)(functools.partial(sent, b_send.at[d, 2]))

    @pl.when(core == 0)
    def _():
        for d in range(NX):
            j = (xx + NX - d) % NX
            pl.when(yy == 1)(functools.partial(sent, f_send.at[j]))
            pl.when(yy == (0 if d < 2 else 2))(functools.partial(sent, f_send.at[NX + j]))

    def share_done(j, _):
        share(j).wait_send()
        return 0

    lax.fori_loop(0, i, share_done, 0)

    def l_done(d, _):
        dest = (i + d) % NI
        l_copy(lev, lall, 0, dest).wait_send()
        l_copy(dwl, dall, 1, dest).wait_send()
        return 0

    lax.fori_loop(1, NI, l_done, 0)
    for d in range(1, NG):
        p_copy(d).wait_send()

    def o_done(q, _):
        for d in range(1, NG):
            o_copy(d, q).wait_send()
        o_own(q).wait()
        return 0

    lax.fori_loop(q_first, nch, o_done, 0)
    for d in range(1, NG):
        src = (g + d) % NG
        rs = row_start(src, n)
        qs = (src * ROWS - rs) // CH

        def o_wait(q, _):
            view = out.at[:, :, 0, pl.ds(pl.multiple_of(rs + q * CH, CH), CH), :]
            pltpu.make_async_copy(view, view, o_recv.at[src, q]).wait()
            return 0

        lax.fori_loop(qs, nch, o_wait, 0)


def shards(coupling, block_mask, levels, dwell, polarization):
    n = levels.shape[1]
    ne = 2 * NG
    vmem = pl.BlockSpec(memory_space=pltpu.VMEM)
    anyw = pl.BlockSpec(memory_space=pl.ANY)
    dma = pltpu.SemaphoreType.DMA
    return pl.pallas_call(
        kernel,
        out_shape=jax.ShapeDtypeStruct(polarization.shape, BF16),
        in_specs=[vmem, vmem, vmem, vmem, anyw],
        out_specs=anyw,
        scratch_shapes=[
            pltpu.VMEM((NI, n, n), BF16),
            pltpu.VMEM((NI, 1, n), F32),
            pltpu.VMEM((NI, 1, n), F32),
            pltpu.VMEM((NI + 1, 2, ne, n), F32),
            pltpu.VMEM((2, ROWS, ne), F32),
            pltpu.VMEM((ne, 2, ROWS, n), BF16),
            pltpu.VMEM((2, ne, ROWS, n), BF16),
            pltpu.VMEM((2, ne, ROWS, n), BF16),
            dma((2, NX)), dma((NI,)),
            dma((NX, NY)), dma((NI,)), dma((NI,)),
            dma((NI,)), dma((NI,)),
            dma((2, NI)), dma((2, NI)),
            dma((NG,)), dma((NG,)),
            dma((NG, ROWS // CH)), dma((NG, ROWS // CH)),
            dma((ROWS // CH,)),
        ],
        compiler_params=pltpu.CompilerParams(
            collective_id=0, has_side_effects=True, vmem_limit_bytes=62 * 1024 * 1024
        ),
        name="gw_sigma",
    )(coupling, jnp.transpose(block_mask, (1, 0, 2)), levels, dwell, polarization)


def solution(mesh):
    return jax.shard_map(
        shards,
        mesh=mesh,
        in_specs=(
            P("cuts", None, None),
            P("cuts", None, None),
            P("cuts", None),
            P("cuts", None),
            P(None, "energy", "cuts", None, None),
        ),
        out_specs=P(None, "energy", "cuts", None, None),
        check_vma=False,
    )
```

```python
import functools
import math

import jax
import jax.numpy as jnp
from jax import lax
from jax.experimental import pallas as pl
from jax.experimental.pallas import tpu as pltpu
from jax.sharding import PartitionSpec as P

MESH = pl.DeviceIdType.MESH
F32 = jnp.float32
BF16 = jnp.bfloat16

NX = 4
NY = 4
NG = 8
NI = NX * NY
ROWS = 96
CH = 16
H0 = 320
SPREAD = (0, 2)
GA = 64
EB = 8
EC = 16


def row_start(g, n):
    return jnp.minimum(g * ROWS, n - ROWS)


def pairwise(parts, value):
    rank = 0
    while parts and parts[-1][0] == rank:
        value = parts.pop()[1] + value
        rank += 1
    parts.append((rank, value))


def collect(parts):
    total = parts.pop()[1]
    while parts:
        total = parts.pop()[1] + total
    return total


def kernel(
    coup, mask, lev, dwl, pol, out,
    call, lall, dall, tab, rph, x, p, sig,
    a_send, a_recv, b_send, b_recv, f_send, c_send, c_recv, l_send, l_recv,
    p_send, p_recv, o_send, o_recv, loc,
):
    n = coup.shape[1]
    ne = x.shape[0]
    nch = ROWS // CH
    g = lax.axis_index("energy")
    i = lax.axis_index("cuts")
    core = g % 2
    yy = i // NX
    xx = i % NX
    r0 = pl.multiple_of(row_start(g, n), 16)

    barrier = pltpu.get_barrier_semaphore()
    for d in range(1, NG):
        pl.semaphore_signal(barrier, 1, device_id=((g + d) % NG, i), device_id_type=MESH)
    for d in range(1, NI):
        pl.semaphore_signal(barrier, 1, device_id=(g, (i + d) % NI), device_id_type=MESH)

    nb = mask.shape[0]
    bw = n // nb
    left = (
        lax.broadcasted_iota(jnp.int32, (n, nb), 0) // bw
        == lax.broadcasted_iota(jnp.int32, (n, nb), 1)
    ).astype(F32).astype(BF16)
    right = (
        lax.broadcasted_iota(jnp.int32, (nb, n), 1) // bw
        == lax.broadcasted_iota(jnp.int32, (nb, n), 0)
    ).astype(F32).astype(BF16)
    small = mask[:, 0, :].astype(F32).astype(BF16)
    wide = jnp.dot(small, right, preferred_element_type=F32).astype(BF16)
    spread = jnp.dot(left, wide, preferred_element_type=F32)
    call[i] = (coup[0].astype(F32) * spread).astype(BF16)

    pl.semaphore_wait(barrier, NG - 1 + NI - 1)

    def share_rows(k):
        return pl.ds(0, H0) if k == 0 else pl.ds(H0, n - H0)

    class Share:
        def __init__(self, make, other=False):
            self.make = make
            self.other = other

        def each(self, act):
            for k in range(2):
                rows = share_rows(1 - k if self.other else k)
                pl.when(core == k)(functools.partial(act, rows))

        def start(self):
            self.each(lambda rows: self.make(rows).start())

        def wait(self):
            self.each(lambda rows: self.make(rows).wait())

        def wait_send(self):
            self.each(lambda rows: self.make(rows).wait_send())

    def send_half(j, dest, ssem, rsem):
        return Share(
            lambda rows: pltpu.make_async_remote_copy(
                call.at[j, rows, :], call.at[j, rows, :], ssem, rsem,
                device_id=(g, dest), device_id_type=MESH,
            )
        )

    def arrived(j, sem, other=False):
        Share(
            lambda rows: pltpu.make_async_copy(
                call.at[j, rows, :], call.at[j, rows, :], sem
            ),
            other,
        ).wait()

    def l_copy(src, dst, k, dest):
        return pltpu.make_async_remote_copy(
            src, dst.at[i], l_send.at[k, dest], l_recv.at[k, i],
            device_id=(g, dest), device_id_type=MESH,
        )

    def l_start(d, _):
        dest = (i + d) % NI
        l_copy(lev, lall, 0, dest).start()
        l_copy(dwl, dall, 1, dest).start()
        return 0

    lax.fori_loop(1, NI, l_start, 0)

    relays = jnp.logical_and(core == 0, yy < NY - 1)

    def row_mate(d):
        return yy * NX + (xx + d) % NX

    for d in (1, 3, 2):
        ok = jnp.logical_or(relays, xx + d < NX)

        @pl.when(ok)
        def _():
            send_half(i, row_mate(d), a_send.at[0, d], a_recv.at[i]).start()

    def column_send(d):
        send_half(i, i + d * NX, a_send.at[1, d], a_recv.at[i]).start()

    for d in (1, 3):
        pl.when(yy + d < NY)(functools.partial(column_send, d))
    pl.when(jnp.logical_and(core == 1, yy + 2 < NY))(functools.partial(column_send, 2))

    def p_copy(d):
        dest = (g + d) % NG
        rd = pl.multiple_of(row_start(dest, n), 16)
        return pltpu.make_async_remote_copy(
            pol.at[:, :, 0, pl.ds(rd, ROWS), :], p.at[:, pl.ds(2 * g, 2)],
            p_send.at[d], p_recv.at[g], device_id=(dest, i), device_id_type=MESH,
        )

    for d in range(1, NG):
        p_copy(d).start()
    p_own = pltpu.make_async_copy(
        pol.at[:, :, 0, pl.ds(r0, ROWS), :], p.at[:, pl.ds(2 * g, 2)], p_recv.at[g]
    )
    p_own.start()

    lall[i] = lev[...]
    dall[i] = dwl[...]

    def l_wait(d, _):
        src = (i + d) % NI
        pltpu.make_async_copy(lall.at[src], lall.at[src], l_recv.at[0, src]).wait()
        pltpu.make_async_copy(dall.at[src], dall.at[src], l_recv.at[1, src]).wait()
        return 0

    lax.fori_loop(1, NI, l_wait, 0)

    tab[0, 0] = jnp.ones((ne, n), F32)
    tab[0, 1] = jnp.zeros((ne, n), F32)
    energy = lax.broadcasted_iota(jnp.int32, (ne, n), 0).astype(F32)

    def tables(j, _):
        phase = (energy - lall[j]) * dall[j]
        tab[j + 1, 0] = jnp.cos(phase)
        tab[j + 1, 1] = jnp.sin(phase)
        return 0

    lax.fori_loop(0, i, tables, 0)

    def share(j):
        return Share(
            lambda rows: pltpu.make_async_remote_copy(
                call.at[j, rows, :], call.at[j, rows, :], c_send.at[j], c_recv.at[j],
                device_id=(g + 1 - 2 * core, i), device_id_type=MESH,
            )
        )

    def own_line(j):
        return jnp.where(
            core == 0, jnp.logical_and(relays, j // NX == yy), j % NX == xx
        )

    def relay(j, dest):
        return send_half(j, dest, f_send.at[j], b_recv.at[j])

    @pl.when(core == 0)
    def _():
        @pl.when(yy == 1)
        def _():
            send_half(i, i - NX, a_send.at[1, 2], b_recv.at[i]).start()

        @pl.when(relays)
        def _():
            for d in (1, 3):
                j = yy * NX + (xx + NX - d) % NX

                arrived(j, a_recv.at[j])

                @pl.when(j < i)
                def _():
                    share(j).start()

                for k in (1, 3):

                    @pl.when(yy + k < NY)
                    def _():
                        send_half(j, i + k * NX, b_send.at[d, k], b_recv.at[j]).start()

                if d == 1:

                    @pl.when(yy == 1)
                    def _():
                        send_half(j, i - NX, b_send.at[d, 2], b_recv.at[j]).start()

        @pl.when(yy == 0)
        def _():
            for d in (0, 1):
                j = NX + (xx + NX - d) % NX
                arrived(j, b_recv.at[j])
                relay(j, i + 3 * NX).start()

    def spread_row(d):
        @pl.when(jnp.logical_and(core == 1, yy >= d))
        def _():
            j = i - d * NX
            arrived(j, a_recv.at[j])
            share(j).start()
            for k in (1, 3, 2):
                send_half(j, row_mate(k), b_send.at[d, k], b_recv.at[j]).start()

    spread_row(1)

    pick = (
        lax.broadcasted_iota(jnp.int32, (ROWS, n), 1)
        == lax.broadcasted_iota(jnp.int32, (ROWS, n), 0) + r0
    )
    col_lev = jnp.sum(jnp.where(pick, lev[...], 0.0), axis=1, keepdims=True)
    col_dwl = jnp.sum(jnp.where(pick, dwl[...], 0.0), axis=1, keepdims=True)
    col_phase = (
        lax.broadcasted_iota(jnp.int32, (ROWS, ne), 1).astype(F32) - col_lev
    ) * col_dwl
    rph[0] = jnp.cos(col_phase)
    rph[1] = jnp.sin(col_phase)

    def init(e, _):
        lane = lax.broadcasted_iota(jnp.int32, (ROWS, ne), 1) == e
        rc = jnp.sum(jnp.where(lane, rph[0], 0.0), axis=1, keepdims=True)
        rs = jnp.sum(jnp.where(lane, rph[1], 0.0), axis=1, keepdims=True)
        c = tab[i, 0, pl.ds(e, 1), :]
        s = tab[i, 1, pl.ds(e, 1), :]
        base = call[i, pl.ds(r0, ROWS), :].astype(F32) * math.sqrt(n / ne)
        x[e, 0] = (base * (rc * c - rs * s)).astype(BF16)
        x[e, 1] = (-base * (rc * s + rs * c)).astype(BF16)
        return 0

    lax.fori_loop(0, ne, init, 0)

    def late():
        j = yy * NX + (xx + 2) % NX

        arrived(j, a_recv.at[j])

        @pl.when(j < i)
        def _():
            share(j).start()

        for k in (1, 3):

            @pl.when(yy + k < NY)
            def _():
                send_half(j, i + k * NX, b_send.at[2, k], b_recv.at[j]).start()

    def passes(j):
        first = jnp.logical_and(yy == 1, j // NX == 0)
        second = jnp.logical_and(yy == 2, jnp.logical_and(j // NX == 1, (xx + NX - j % NX) % NX >= 2))
        return jnp.logical_and(core == 0, jnp.logical_or(first, second))

    def take(j):
        @pl.when(jnp.logical_not(own_line(j)))
        def _():
            direct = jnp.where(
                core == 0,
                jnp.logical_or(
                    j // NX == yy,
                    jnp.logical_and(j % NX == xx, yy - j // NX != 2),
                ),
                j // NX == yy,
            )

            @pl.when(direct)
            def _():
                arrived(j, a_recv.at[j])

            @pl.when(jnp.logical_not(direct))
            def _():
                arrived(j, b_recv.at[j])

            @pl.when(passes(j))
            def _():
                relay(j, i + NX).start()

            share(j).start()

    @pl.when(jnp.logical_and(core == 0, i == 0))
    def _():
        late()

    @pl.when(i > 0)
    def _():
        take(i - 1)


    def block(j, b, rows, count):
        first, size = rows
        z = x[pl.ds(b * count, count), :, first : first + size, :]
        z = z.reshape(count * 2 * size, n)
        r = jnp.dot(z, call[j], preferred_element_type=F32)
        for k in range(count):
            e = b * count + k
            c = tab[j, 0, pl.ds(e, 1), :]
            s = tab[j, 1, pl.ds(e, 1), :]
            re = r[2 * k * size : (2 * k + 1) * size]
            im = r[(2 * k + 1) * size : (2 * k + 2) * size]
            x[e, 0, first : first + size, :] = (re * c + im * s).astype(BF16)
            x[e, 1, first : first + size, :] = (im * c - re * s).astype(BF16)

    def chain(q, _):
        j = i - 1 - q
        arrived(j, c_recv.at[j], other=True)

        def part(b, _):
            block(j, b, (0, GA), EB)

            @pl.when(b == 0)
            def _():
                @pl.when(jnp.logical_and(relays, q == 0))
                def _():
                    late()

                for d in range(2, NY):
                    pl.when(q == SPREAD[d - 2])(functools.partial(spread_row, d))

                @pl.when(j > 0)
                def _():
                    take(j - 1)

            return 0

        lax.fori_loop(0, ne // EB, part, 0)
        return 0

    lax.fori_loop(0, i, chain, 0)

    def chain_rest(q, _):
        j = i - 1 - q

        def part(b, _):
            block(j, b, (GA, ROWS - GA), EC)
            return 0

        lax.fori_loop(0, ne // EC, part, 0)
        return 0

    p_own.wait()
    for d in range(1, NG):
        src = (g + NG - d) % NG
        view = p.at[:, pl.ds(2 * src, 2)]
        pltpu.make_async_copy(view, view, p_recv.at[src]).wait()

    def o_copy(d, q):
        dest = (g + d) % NG
        rows = pl.ds(pl.multiple_of(r0 + q * CH, CH), CH)
        return pltpu.make_async_remote_copy(
            sig.at[:, pl.ds(2 * dest, 2), pl.ds(pl.multiple_of(q * CH, CH), CH), :],
            out.at[:, :, 0, rows, :],
            o_send.at[d, q], o_recv.at[g, q], device_id=(dest, i), device_id_type=MESH,
        )

    def o_own(q):
        rows = pl.ds(pl.multiple_of(r0 + q * CH, CH), CH)
        return pltpu.make_async_copy(
            sig.at[:, pl.ds(2 * g, 2), pl.ds(pl.multiple_of(q * CH, CH), CH), :],
            out.at[:, :, 0, rows, :], loc.at[q],
        )

    q_first = (g * ROWS - r0) // CH

    def chunk(q, _):
        rows = pl.ds(pl.multiple_of(q * CH, CH), CH)

        def tile(lane):
            ga = [x[e, 0, rows, lane] for e in range(ne)]
            gb = [x[e, 1, rows, lane] for e in range(ne)]
            for e in range(ne):
                res, ims = [], []
                for w in range(e + 1):
                    pr = p[0, w, rows, lane]
                    pi = p[1, w, rows, lane]
                    pairwise(res, pr * ga[e - w] - pi * gb[e - w])
                    pairwise(ims, pr * gb[e - w] + pi * ga[e - w])
                sig[0, e, rows, lane] = collect(res)
                sig[1, e, rows, lane] = collect(ims)

        def whole(t, _):
            tile(pl.ds(pl.multiple_of(t * 128, 128), 128))
            return 0

        lax.fori_loop(0, n // 128, whole, 0)
        if n % 128:
            tile(pl.ds(n - n % 128, n % 128))
        for d in range(1, NG):
            o_copy(d, q).start()
        o_own(q).start()
        return 0

    lax.fori_loop(q_first, GA // CH, chunk, 0)
    lax.fori_loop(0, i, chain_rest, 0)
    lax.fori_loop(GA // CH, nch, chunk, 0)

    for d in range(1, NX):
        ok = jnp.logical_or(relays, xx + d < NX)

        @pl.when(ok)
        def _():
            send_half(i, row_mate(d), a_send.at[0, d], a_recv.at[i]).wait_send()

    def sent(sem):
        send_half(i, i, sem, a_recv.at[i]).wait_send()

    for d in (1, 3):
        pl.when(yy + d < NY)(functools.partial(sent, a_send.at[1, d]))
    ok = jnp.where(core == 1, yy + 2 < NY, yy == 1)
    pl.when(ok)(functools.partial(sent, a_send.at[1, 2]))
    for d in range(1, NX):
        for k in (1, 3):
            ok = jnp.where(core == 0, yy + k < NY, yy >= d)
            pl.when(ok)(functools.partial(sent, b_send.at[d, k]))
        ok = jnp.where(core == 0, yy == 1 if d == 1 else False, yy >= d)
        pl.when(ok)(functools.partial(sent, b_send.at[d, 2]))

    @pl.when(core == 0)
    def _():
        for d in range(NX):
            j = (xx + NX - d) % NX
            pl.when(yy == 1)(functools.partial(sent, f_send.at[j]))
            pl.when(yy == (0 if d < 2 else 2))(functools.partial(sent, f_send.at[NX + j]))

    def share_done(j, _):
        share(j).wait_send()
        return 0

    lax.fori_loop(0, i, share_done, 0)

    def l_done(d, _):
        dest = (i + d) % NI
        l_copy(lev, lall, 0, dest).wait_send()
        l_copy(dwl, dall, 1, dest).wait_send()
        return 0

    lax.fori_loop(1, NI, l_done, 0)
    for d in range(1, NG):
        p_copy(d).wait_send()

    def o_done(q, _):
        for d in range(1, NG):
            o_copy(d, q).wait_send()
        o_own(q).wait()
        return 0

    lax.fori_loop(q_first, nch, o_done, 0)
    for d in range(1, NG):
        src = (g + d) % NG
        rs = row_start(src, n)
        qs = (src * ROWS - rs) // CH

        def o_wait(q, _):
            view = out.at[:, :, 0, pl.ds(pl.multiple_of(rs + q * CH, CH), CH), :]
            pltpu.make_async_copy(view, view, o_recv.at[src, q]).wait()
            return 0

        lax.fori_loop(qs, nch, o_wait, 0)


def shards(coupling, block_mask, levels, dwell, polarization):
    n = levels.shape[1]
    ne = 2 * NG
    vmem = pl.BlockSpec(memory_space=pltpu.VMEM)
    anyw = pl.BlockSpec(memory_space=pl.ANY)
    dma = pltpu.SemaphoreType.DMA
    return pl.pallas_call(
        kernel,
        out_shape=jax.ShapeDtypeStruct(polarization.shape, BF16),
        in_specs=[vmem, vmem, vmem, vmem, anyw],
        out_specs=anyw,
        scratch_shapes=[
            pltpu.VMEM((NI, n, n), BF16),
            pltpu.VMEM((NI, 1, n), F32),
            pltpu.VMEM((NI, 1, n), F32),
            pltpu.VMEM((NI + 1, 2, ne, n), F32),
            pltpu.VMEM((2, ROWS, ne), F32),
            pltpu.VMEM((ne, 2, ROWS, n), BF16),
            pltpu.VMEM((2, ne, ROWS, n), BF16),
            pltpu.VMEM((2, ne, ROWS, n), BF16),
            dma((2, NX)), dma((NI,)),
            dma((NX, NY)), dma((NI,)), dma((NI,)),
            dma((NI,)), dma((NI,)),
            dma((2, NI)), dma((2, NI)),
            dma((NG,)), dma((NG,)),
            dma((NG, ROWS // CH)), dma((NG, ROWS // CH)),
            dma((ROWS // CH,)),
        ],
        compiler_params=pltpu.CompilerParams(
            collective_id=0, has_side_effects=True, vmem_limit_bytes=62 * 1024 * 1024
        ),
        name="gw_sigma",
    )(coupling, jnp.transpose(block_mask, (1, 0, 2)), levels, dwell, polarization)


def solution(mesh):
    return jax.shard_map(
        shards,
        mesh=mesh,
        in_specs=(
            P("cuts", None, None),
            P("cuts", None, None),
            P("cuts", None),
            P("cuts", None),
            P(None, "energy", "cuts", None, None),
        ),
        out_specs=P(None, "energy", "cuts", None, None),
        check_vma=False,
    )
```

```python
import functools
import math

import jax
import jax.numpy as jnp
from jax import lax
from jax.experimental import pallas as pl
from jax.experimental.pallas import tpu as pltpu
from jax.sharding import PartitionSpec as P

MESH = pl.DeviceIdType.MESH
F32 = jnp.float32
BF16 = jnp.bfloat16

NX = 4
NY = 4
NG = 8
NI = NX * NY
ROWS = 96
CH = 16
H0 = 320
SPREAD = (0, 2)
GA = 64
EB = 8
EC = 16


def row_start(g, n):
    return jnp.minimum(g * ROWS, n - ROWS)


def pairwise(parts, value):
    rank = 0
    while parts and parts[-1][0] == rank:
        value = parts.pop()[1] + value
        rank += 1
    parts.append((rank, value))


def collect(parts):
    total = parts.pop()[1]
    while parts:
        total = parts.pop()[1] + total
    return total


def kernel(
    coup, mask, lev, dwl, pol, out,
    call, lall, dall, tab, rph, x, p, sig,
    a_send, a_recv, b_send, b_recv, f_send, c_send, c_recv, l_send, l_recv,
    p_send, p_recv, o_send, o_recv, loc,
):
    n = coup.shape[1]
    ne = x.shape[0]
    nch = ROWS // CH
    g = lax.axis_index("energy")
    i = lax.axis_index("cuts")
    core = g % 2
    yy = i // NX
    xx = i % NX
    r0 = pl.multiple_of(row_start(g, n), 16)

    barrier = pltpu.get_barrier_semaphore()
    for d in range(1, NG):
        pl.semaphore_signal(barrier, 1, device_id=((g + d) % NG, i), device_id_type=MESH)
    for d in range(1, NI):
        pl.semaphore_signal(barrier, 1, device_id=(g, (i + d) % NI), device_id_type=MESH)

    nb = mask.shape[0]
    bw = n // nb
    left = (
        lax.broadcasted_iota(jnp.int32, (n, nb), 0) // bw
        == lax.broadcasted_iota(jnp.int32, (n, nb), 1)
    ).astype(F32).astype(BF16)
    right = (
        lax.broadcasted_iota(jnp.int32, (nb, n), 1) // bw
        == lax.broadcasted_iota(jnp.int32, (nb, n), 0)
    ).astype(F32).astype(BF16)
    small = mask[:, 0, :].astype(F32).astype(BF16)
    wide = jnp.dot(small, right, preferred_element_type=F32).astype(BF16)
    spread = jnp.dot(left, wide, preferred_element_type=F32)
    call[i] = (coup[0].astype(F32) * spread).astype(BF16)

    pl.semaphore_wait(barrier, NG - 1 + NI - 1)

    def share_rows(k):
        return pl.ds(0, H0) if k == 0 else pl.ds(H0, n - H0)

    class Share:
        def __init__(self, make, other=False):
            self.make = make
            self.other = other

        def each(self, act):
            for k in range(2):
                rows = share_rows(1 - k if self.other else k)
                pl.when(core == k)(functools.partial(act, rows))

        def start(self):
            self.each(lambda rows: self.make(rows).start())

        def wait(self):
            self.each(lambda rows: self.make(rows).wait())

        def wait_send(self):
            self.each(lambda rows: self.make(rows).wait_send())

    def send_half(j, dest, ssem, rsem):
        return Share(
            lambda rows: pltpu.make_async_remote_copy(
                call.at[j, rows, :], call.at[j, rows, :], ssem, rsem,
                device_id=(g, dest), device_id_type=MESH,
            )
        )

    def arrived(j, sem, other=False):
        Share(
            lambda rows: pltpu.make_async_copy(
                call.at[j, rows, :], call.at[j, rows, :], sem
            ),
            other,
        ).wait()

    def l_copy(src, dst, k, dest):
        return pltpu.make_async_remote_copy(
            src, dst.at[i], l_send.at[k, dest], l_recv.at[k, i],
            device_id=(g, dest), device_id_type=MESH,
        )

    def l_start(d, _):
        dest = (i + d) % NI
        l_copy(lev, lall, 0, dest).start()
        l_copy(dwl, dall, 1, dest).start()
        return 0

    lax.fori_loop(1, NI, l_start, 0)

    relays = jnp.logical_and(core == 0, yy < NY - 1)

    def row_mate(d):
        return yy * NX + (xx + d) % NX

    for d in (1, 3, 2):
        ok = jnp.logical_or(relays, xx + d < NX)

        @pl.when(ok)
        def _():
            send_half(i, row_mate(d), a_send.at[0, d], a_recv.at[i]).start()

    def column_send(d):
        send_half(i, i + d * NX, a_send.at[1, d], a_recv.at[i]).start()

    for d in (1, 3):
        pl.when(yy + d < NY)(functools.partial(column_send, d))
    pl.when(jnp.logical_and(core == 1, yy + 2 < NY))(functools.partial(column_send, 2))

    def p_copy(d):
        dest = (g + d) % NG
        rd = pl.multiple_of(row_start(dest, n), 16)
        return pltpu.make_async_remote_copy(
            pol.at[:, :, 0, pl.ds(rd, ROWS), :], p.at[:, pl.ds(2 * g, 2)],
            p_send.at[d], p_recv.at[g], device_id=(dest, i), device_id_type=MESH,
        )

    for d in range(1, NG):
        p_copy(d).start()
    p_own = pltpu.make_async_copy(
        pol.at[:, :, 0, pl.ds(r0, ROWS), :], p.at[:, pl.ds(2 * g, 2)], p_recv.at[g]
    )
    p_own.start()

    lall[i] = lev[...]
    dall[i] = dwl[...]

    def l_wait(d, _):
        src = (i + d) % NI
        pltpu.make_async_copy(lall.at[src], lall.at[src], l_recv.at[0, src]).wait()
        pltpu.make_async_copy(dall.at[src], dall.at[src], l_recv.at[1, src]).wait()
        return 0

    lax.fori_loop(1, NI, l_wait, 0)

    tab[0, 0] = jnp.ones((ne, n), F32)
    tab[0, 1] = jnp.zeros((ne, n), F32)
    energy = lax.broadcasted_iota(jnp.int32, (ne, n), 0).astype(F32)

    def tables(j, _):
        phase = (energy - lall[j]) * dall[j]
        tab[j + 1, 0] = jnp.cos(phase)
        tab[j + 1, 1] = jnp.sin(phase)
        return 0

    lax.fori_loop(0, i, tables, 0)

    def share(j):
        return Share(
            lambda rows: pltpu.make_async_remote_copy(
                call.at[j, rows, :], call.at[j, rows, :], c_send.at[j], c_recv.at[j],
                device_id=(g + 1 - 2 * core, i), device_id_type=MESH,
            )
        )

    def own_line(j):
        return jnp.where(
            core == 0, jnp.logical_and(relays, j // NX == yy), j % NX == xx
        )

    def relay(j, dest):
        return send_half(j, dest, f_send.at[j], b_recv.at[j])

    @pl.when(core == 0)
    def _():
        @pl.when(yy == 1)
        def _():
            send_half(i, i - NX, a_send.at[1, 2], b_recv.at[i]).start()

        @pl.when(relays)
        def _():
            for d in (1, 3):
                j = yy * NX + (xx + NX - d) % NX

                arrived(j, a_recv.at[j])

                @pl.when(j < i)
                def _():
                    share(j).start()

                send_half(j, i + NX, b_send.at[d, 1], b_recv.at[j]).start()

                if d == 1:

                    @pl.when(yy == 1)
                    def _():
                        send_half(j, i - NX, b_send.at[d, 2], b_recv.at[j]).start()

        @pl.when(yy == 0)
        def _():
            for d in (0, 1):
                j = NX + (xx + NX - d) % NX
                arrived(j, b_recv.at[j])
                relay(j, i + 3 * NX).start()

            for d in (1, 3):
                j = (xx + NX - d) % NX
                send_half(j, i + 3 * NX, b_send.at[d, 3], b_recv.at[j]).start()

    def spread_row(d):
        @pl.when(jnp.logical_and(core == 1, yy >= d))
        def _():
            j = i - d * NX
            arrived(j, a_recv.at[j])
            share(j).start()
            for k in (1, 3, 2):
                send_half(j, row_mate(k), b_send.at[d, k], b_recv.at[j]).start()

    spread_row(1)

    pick = (
        lax.broadcasted_iota(jnp.int32, (ROWS, n), 1)
        == lax.broadcasted_iota(jnp.int32, (ROWS, n), 0) + r0
    )
    col_lev = jnp.sum(jnp.where(pick, lev[...], 0.0), axis=1, keepdims=True)
    col_dwl = jnp.sum(jnp.where(pick, dwl[...], 0.0), axis=1, keepdims=True)
    col_phase = (
        lax.broadcasted_iota(jnp.int32, (ROWS, ne), 1).astype(F32) - col_lev
    ) * col_dwl
    rph[0] = jnp.cos(col_phase)
    rph[1] = jnp.sin(col_phase)

    def init(e, _):
        lane = lax.broadcasted_iota(jnp.int32, (ROWS, ne), 1) == e
        rc = jnp.sum(jnp.where(lane, rph[0], 0.0), axis=1, keepdims=True)
        rs = jnp.sum(jnp.where(lane, rph[1], 0.0), axis=1, keepdims=True)
        c = tab[i, 0, pl.ds(e, 1), :]
        s = tab[i, 1, pl.ds(e, 1), :]
        base = call[i, pl.ds(r0, ROWS), :].astype(F32) * math.sqrt(n / ne)
        x[e, 0] = (base * (rc * c - rs * s)).astype(BF16)
        x[e, 1] = (-base * (rc * s + rs * c)).astype(BF16)
        return 0

    lax.fori_loop(0, ne, init, 0)

    def late():
        j = yy * NX + (xx + 2) % NX

        arrived(j, a_recv.at[j])

        @pl.when(j < i)
        def _():
            share(j).start()

        for k in (1, 3):

            @pl.when(yy + k < NY)
            def _():
                send_half(j, i + k * NX, b_send.at[2, k], b_recv.at[j]).start()

    def passes(j):
        first = jnp.logical_and(yy == 1, j // NX == 0)
        second = jnp.logical_and(yy == 2, jnp.logical_and(j // NX == 1, (xx + NX - j % NX) % NX >= 2))
        return jnp.logical_and(core == 0, jnp.logical_or(first, second))

    def take(j):
        @pl.when(jnp.logical_not(own_line(j)))
        def _():
            direct = jnp.where(
                core == 0,
                jnp.logical_or(
                    j // NX == yy,
                    jnp.logical_and(j % NX == xx, yy - j // NX != 2),
                ),
                j // NX == yy,
            )

            @pl.when(direct)
            def _():
                arrived(j, a_recv.at[j])

            @pl.when(jnp.logical_not(direct))
            def _():
                arrived(j, b_recv.at[j])

            @pl.when(passes(j))
            def _():
                relay(j, i + NX).start()

            share(j).start()

    @pl.when(jnp.logical_and(core == 0, i == 0))
    def _():
        late()

    @pl.when(i > 0)
    def _():
        take(i - 1)


    def block(j, b, rows, count):
        first, size = rows
        z = x[pl.ds(b * count, count), :, first : first + size, :]
        z = z.reshape(count * 2 * size, n)
        r = jnp.dot(z, call[j], preferred_element_type=F32)
        for k in range(count):
            e = b * count + k
            c = tab[j, 0, pl.ds(e, 1), :]
            s = tab[j, 1, pl.ds(e, 1), :]
            re = r[2 * k * size : (2 * k + 1) * size]
            im = r[(2 * k + 1) * size : (2 * k + 2) * size]
            x[e, 0, first : first + size, :] = (re * c + im * s).astype(BF16)
            x[e, 1, first : first + size, :] = (im * c - re * s).astype(BF16)

    def chain(q, _):
        j = i - 1 - q
        arrived(j, c_recv.at[j], other=True)

        def part(b, _):
            block(j, b, (0, GA), EB)

            @pl.when(b == 0)
            def _():
                @pl.when(jnp.logical_and(relays, q == 0))
                def _():
                    late()

                for d in range(2, NY):
                    pl.when(q == SPREAD[d - 2])(functools.partial(spread_row, d))

                @pl.when(j > 0)
                def _():
                    take(j - 1)

            return 0

        lax.fori_loop(0, ne // EB, part, 0)
        return 0

    lax.fori_loop(0, i, chain, 0)

    def chain_rest(q, _):
        j = i - 1 - q

        def part(b, _):
            block(j, b, (GA, ROWS - GA), EC)
            return 0

        lax.fori_loop(0, ne // EC, part, 0)
        return 0

    p_own.wait()
    for d in range(1, NG):
        src = (g + NG - d) % NG
        view = p.at[:, pl.ds(2 * src, 2)]
        pltpu.make_async_copy(view, view, p_recv.at[src]).wait()

    def o_copy(d, q):
        dest = (g + d) % NG
        rows = pl.ds(pl.multiple_of(r0 + q * CH, CH), CH)
        return pltpu.make_async_remote_copy(
            sig.at[:, pl.ds(2 * dest, 2), pl.ds(pl.multiple_of(q * CH, CH), CH), :],
            out.at[:, :, 0, rows, :],
            o_send.at[d, q], o_recv.at[g, q], device_id=(dest, i), device_id_type=MESH,
        )

    def o_own(q):
        rows = pl.ds(pl.multiple_of(r0 + q * CH, CH), CH)
        return pltpu.make_async_copy(
            sig.at[:, pl.ds(2 * g, 2), pl.ds(pl.multiple_of(q * CH, CH), CH), :],
            out.at[:, :, 0, rows, :], loc.at[q],
        )

    q_first = (g * ROWS - r0) // CH

    def chunk(q, _):
        rows = pl.ds(pl.multiple_of(q * CH, CH), CH)

        def tile(lane):
            ga = [x[e, 0, rows, lane] for e in range(ne)]
            gb = [x[e, 1, rows, lane] for e in range(ne)]
            for e in range(ne):
                res, ims = [], []
                for w in range(e + 1):
                    pr = p[0, w, rows, lane]
                    pi = p[1, w, rows, lane]
                    pairwise(res, pr * ga[e - w] - pi * gb[e - w])
                    pairwise(ims, pr * gb[e - w] + pi * ga[e - w])
                sig[0, e, rows, lane] = collect(res)
                sig[1, e, rows, lane] = collect(ims)

        def whole(t, _):
            tile(pl.ds(pl.multiple_of(t * 128, 128), 128))
            return 0

        lax.fori_loop(0, n // 128, whole, 0)
        if n % 128:
            tile(pl.ds(n - n % 128, n % 128))
        for d in range(1, NG):
            o_copy(d, q).start()
        o_own(q).start()
        return 0

    lax.fori_loop(q_first, GA // CH, chunk, 0)
    lax.fori_loop(0, i, chain_rest, 0)
    lax.fori_loop(GA // CH, nch, chunk, 0)

    for d in range(1, NX):
        ok = jnp.logical_or(relays, xx + d < NX)

        @pl.when(ok)
        def _():
            send_half(i, row_mate(d), a_send.at[0, d], a_recv.at[i]).wait_send()

    def sent(sem):
        send_half(i, i, sem, a_recv.at[i]).wait_send()

    for d in (1, 3):
        pl.when(yy + d < NY)(functools.partial(sent, a_send.at[1, d]))
    ok = jnp.where(core == 1, yy + 2 < NY, yy == 1)
    pl.when(ok)(functools.partial(sent, a_send.at[1, 2]))
    for d in range(1, NX):
        for k in (1, 3):
            ok = jnp.where(core == 0, yy + k < NY, yy >= d)
            pl.when(ok)(functools.partial(sent, b_send.at[d, k]))
        ok = jnp.where(core == 0, yy == 1 if d == 1 else False, yy >= d)
        pl.when(ok)(functools.partial(sent, b_send.at[d, 2]))

    @pl.when(core == 0)
    def _():
        for d in range(NX):
            j = (xx + NX - d) % NX
            pl.when(yy == 1)(functools.partial(sent, f_send.at[j]))
            pl.when(yy == (0 if d < 2 else 2))(functools.partial(sent, f_send.at[NX + j]))

    def share_done(j, _):
        share(j).wait_send()
        return 0

    lax.fori_loop(0, i, share_done, 0)

    def l_done(d, _):
        dest = (i + d) % NI
        l_copy(lev, lall, 0, dest).wait_send()
        l_copy(dwl, dall, 1, dest).wait_send()
        return 0

    lax.fori_loop(1, NI, l_done, 0)
    for d in range(1, NG):
        p_copy(d).wait_send()

    def o_done(q, _):
        for d in range(1, NG):
            o_copy(d, q).wait_send()
        o_own(q).wait()
        return 0

    lax.fori_loop(q_first, nch, o_done, 0)
    for d in range(1, NG):
        src = (g + d) % NG
        rs = row_start(src, n)
        qs = (src * ROWS - rs) // CH

        def o_wait(q, _):
            view = out.at[:, :, 0, pl.ds(pl.multiple_of(rs + q * CH, CH), CH), :]
            pltpu.make_async_copy(view, view, o_recv.at[src, q]).wait()
            return 0

        lax.fori_loop(qs, nch, o_wait, 0)


def shards(coupling, block_mask, levels, dwell, polarization):
    n = levels.shape[1]
    ne = 2 * NG
    vmem = pl.BlockSpec(memory_space=pltpu.VMEM)
    anyw = pl.BlockSpec(memory_space=pl.ANY)
    dma = pltpu.SemaphoreType.DMA
    return pl.pallas_call(
        kernel,
        out_shape=jax.ShapeDtypeStruct(polarization.shape, BF16),
        in_specs=[vmem, vmem, vmem, vmem, pl.BlockSpec(memory_space=pltpu.HBM)],
        out_specs=anyw,
        scratch_shapes=[
            pltpu.VMEM((NI, n, n), BF16),
            pltpu.VMEM((NI, 1, n), F32),
            pltpu.VMEM((NI, 1, n), F32),
            pltpu.VMEM((NI + 1, 2, ne, n), F32),
            pltpu.VMEM((2, ROWS, ne), F32),
            pltpu.VMEM((ne, 2, ROWS, n), BF16),
            pltpu.VMEM((2, ne, ROWS, n), BF16),
            pltpu.VMEM((2, ne, ROWS, n), BF16),
            dma((2, NX)), dma((NI,)),
            dma((NX, NY)), dma((NI,)), dma((NI,)),
            dma((NI,)), dma((NI,)),
            dma((2, NI)), dma((2, NI)),
            dma((NG,)), dma((NG,)),
            dma((NG, ROWS // CH)), dma((NG, ROWS // CH)),
            dma((ROWS // CH,)),
        ],
        compiler_params=pltpu.CompilerParams(
            collective_id=0, has_side_effects=True, vmem_limit_bytes=48 * 1024 * 1024
        ),
        name="gw_sigma",
    )(coupling, jnp.transpose(block_mask, (1, 0, 2)), levels, dwell, polarization)


def solution(mesh):
    return jax.shard_map(
        shards,
        mesh=mesh,
        in_specs=(
            P("cuts", None, None),
            P("cuts", None, None),
            P("cuts", None),
            P("cuts", None),
            P(None, "energy", "cuts", None, None),
        ),
        out_specs=P(None, "energy", "cuts", None, None),
        check_vma=False,
    )
```
